256 devices in a mesh: req: 16 (over y, x), kv: 8 (over z), blk: 2 (over core).
Axes of the slice: x: 4, y: 4, z: 8, core: 2. Of those that a mesh axis runs over, the one named last changes fastest.
Arguments:
- x_resid: bfloat16 [16, 256, 5120], P('req', ('kv', 'blk')), may hold values from -54 to 54
- q_new: bfloat16 [16, 256, 4096], P('req', None, 'kv'), may hold values from -36 to 36
- k_new: bfloat16 [16, 256, 1024], P('req', None, 'kv'), may hold values from -6 to 12
- v_new: bfloat16 [16, 256, 1024], P('req', None, 'kv'), may hold values from -24 to 24
- k_cache: bfloat16 [16, 8, 64, 128, 128], P('req', 'kv', 'blk'), may hold values from -6 to 12
- v_cache: bfloat16 [16, 8, 64, 128, 128], P('req', 'kv', 'blk'), may hold values from -24 to 24
- cache_len: int32 [16], P('req'), may hold values from 1 to 7936, as said below
- page_table: int32 [16, 64], P('req'), may hold values from 0 to 63, as said below
- wo: bfloat16 [4096, 5120], P(('kv', 'blk')), may hold values from -0.09375 to 0.09375
- norm_gain: bfloat16 [5120], replicated, may hold values from 0.099609375 to 1.8984375
- w_gate: bfloat16 [5120, 7168], P('req', ('kv', 'blk')), may hold values from -0.078125 to 0.078125
- w_up: bfloat16 [5120, 7168], P('req', ('kv', 'blk')), may hold values from -0.078125 to 0.078125
- w_down: bfloat16 [7168, 5120], P(('kv', 'blk'), 'req'), may hold values from -0.0625 to 0.0625
Outputs:
- layer_out: bfloat16 [16, 256, 5120], P('req', ('kv', 'blk'))
- k_cache_out: bfloat16 [16, 8, 64, 128, 128], P('req', 'kv', 'blk')
- v_cache_out: bfloat16 [16, 8, 64, 128, 128], P('req', 'kv', 'blk')
The draws below stay inside these ranges and needn't reach their ends.
Inputs may be any that keep to these rules, and one draw needn't show every extreme that they name: `cache_len`: at least one request has the largest length. `page_table`: each row is a permutation of 0 to 63.
All inputs are finite; a program needn't handle non-finite values.
Results may differ from the reference program's by a relative error of at most 0.0095.
Values may be sent and summed in bfloat16 or wider, within the bound.
A program may use at most 128 MiB of HBM per device.

```python
import math
import jax
import jax.numpy as jnp
from jax import lax

D = 5120
HD = 128
GROUP = 4
FFW = 7168
C = 256
PAGE = 128
SLOTS = 32
KVH = 8
HEADS = 32
NPAGE = 64
REQS = 16
N_BLK = 2


def draw_q_new(key, part):
    first_key = jax.random.fold_in(key, 0)
    base = jnp.clip(jax.random.normal(first_key, (REQS, C, HEADS, HD), jnp.float32), -6.0, 6.0)
    return base.reshape(REQS, C, HEADS * HD).astype(jnp.bfloat16)


def draw_k_new(key, part):
    first_key = jax.random.fold_in(key, 0)
    base = jnp.clip(jax.random.normal(first_key, (REQS, C, KVH, HD), jnp.float32), -6.0, 6.0)
    return base.reshape(REQS, C, KVH * HD).astype(jnp.bfloat16)


def draw_k_cache(key, part):
    first_key = jax.random.fold_in(key, 0)
    base = jnp.clip(jax.random.normal(first_key, (REQS, KVH, NPAGE, PAGE, HD), jnp.float32), -6.0, 6.0)
    return base.astype(jnp.bfloat16)


def draw_x_resid(key, part):
    first_key, second_key, third_key = jax.random.split(key, 3)
    base = jnp.clip(jax.random.normal(first_key, (REQS, C, D), jnp.float32), -6.0, 6.0)
    row_scale = jnp.exp(jax.random.uniform(second_key, (REQS, C, 1), jnp.float32, jnp.log(0.3), jnp.log(3.0)))
    column_scale = jnp.exp(jax.random.uniform(third_key, (D,), jnp.float32, jnp.log(0.3), jnp.log(3.0)))
    return (base * row_scale * column_scale).astype(jnp.bfloat16)


def draw_cache_len(key, part):
    keys_all = jax.random.split(key, 4)
    longest = NPAGE * PAGE - C
    first_draw = jax.random.randint(keys_all[0], (REQS,), 0, longest + 1)
    second_draw = jax.random.randint(keys_all[1], (REQS,), 0, longest + 1)
    third_draw = jax.random.randint(keys_all[2], (REQS,), 0, longest + 1)
    lengths = first_draw * second_draw // longest * third_draw // longest
    lengths = jnp.maximum(lengths, 1)
    picked = jax.random.randint(keys_all[3], (), 0, REQS)
    return jnp.where(jnp.arange(REQS) == picked, longest, lengths).astype(jnp.int32)


def draw_page_table(key, part):
    request_keys = jax.random.split(key, REQS)
    return jax.vmap(lambda single: jax.random.permutation(single, NPAGE))(request_keys).astype(jnp.int32)


def level_of(key, extent, cuts, least, largest):
    gain = 1.0
    for position, shards_of in cuts:
        draws = jax.random.uniform(jax.random.fold_in(jax.random.fold_in(key, 6), position), (shards_of,), jnp.float32, least / len(cuts), largest / len(cuts))
        gain = gain * jnp.repeat(jnp.exp(draws), extent[position] // shards_of).reshape((-1,) + (1,) * (len(extent) - 1 - position))
    return gain


def scatter_about(key, shape, scale, limit, shards=(), kind=jnp.bfloat16):
    array = jax.random.normal(key, shape, jnp.float32) * scale
    if len(shards) > 0:
        array = level_of(key, shape, shards, -0.22, 0.18) * array
    return jnp.clip(array, min=-limit, max=limit).astype(kind)


def setup_inputs(seed: int = 0) -> dict:
    key_of = jax.random.split(jax.random.key(seed), 14)
    return {
        "x_resid": draw_x_resid(jax.random.fold_in(key_of[13], 71), 0),
        "q_new": draw_q_new(jax.random.fold_in(key_of[13], 71), 0),
        "k_new": draw_k_new(jax.random.fold_in(key_of[13], 71), 0),
        "v_new": scatter_about(key_of[3], (REQS, C, KVH * HD), 4.0, 24.0, ((0, 16), (2, 8))),
        "k_cache": draw_k_cache(jax.random.fold_in(key_of[13], 71), 0),
        "v_cache": scatter_about(key_of[5], (REQS, KVH, NPAGE, PAGE, HD), 4.0, 24.0, ((0, 16), (1, 8), (2, 2))),
        "cache_len": draw_cache_len(jax.random.fold_in(key_of[13], 71), 0),
        "page_table": draw_page_table(jax.random.fold_in(key_of[13], 71), 0),
        "wo": scatter_about(key_of[8], (HEADS * HD, D), (HEADS * HD) ** -0.5, 0.09375, ((0, 16),)),
        "norm_gain": jnp.clip(1.0 + 0.18 * jax.random.normal(key_of[9], (D,), jnp.float32), 0.099609375, 1.8984375).astype(jnp.bfloat16),
        "w_gate": scatter_about(key_of[10], (D, FFW), D ** -0.5, 0.078125, ((0, 16), (1, 16))),
        "w_up": scatter_about(key_of[11], (D, FFW), D ** -0.5, 0.078125, ((0, 16), (1, 16))),
        "w_down": scatter_about(key_of[12], (FFW, D), FFW ** -0.5, 0.0625, ((0, 16), (1, 16))),
    }


def rotate(field, positions):
    half_width = field.shape[-1] // 2
    pair_index = jnp.arange(half_width, dtype=jnp.float32)
    frequency = jnp.power(1000000.0, -2.0 * pair_index / field.shape[-1])
    angles = positions.astype(jnp.float32)[:, None] * frequency[None, :]
    cosine = jnp.cos(angles)
    sine_part = jnp.sin(angles)
    lower_half = field[..., :half_width]
    upper_half = field[..., half_width:]
    return jnp.concatenate([lower_half * cosine - upper_half * sine_part, upper_half * cosine + lower_half * sine_part], axis=-1)

def attend_head(queries, key_rows, value_rows, key_position, query_position):
    key_blocks = key_rows.reshape(N_BLK, SLOTS * PAGE, HD).astype(jnp.float32)
    value_blocks = value_rows.reshape(N_BLK, SLOTS * PAGE, HD).astype(jnp.float32)
    position_blocks = key_position.reshape(N_BLK, 1, 1, SLOTS * PAGE)
    scores = jnp.einsum('gcd,bsd->bgcs', queries.astype(jnp.float32), key_blocks) * (1.0 / math.sqrt(HD))
    allowed = position_blocks <= query_position[None, None, :, None]
    masked = jnp.where(allowed, scores, -1e+30)
    block_max = lax.optimization_barrier(jnp.max(masked, axis=-1))
    weights = jnp.where(allowed, jnp.exp(masked - block_max[..., None]), 0.0).astype(jnp.bfloat16)
    block_total = lax.optimization_barrier(jnp.sum(weights.astype(jnp.float32), axis=-1))
    block_out = jnp.einsum('bgcs,bsd->bgcd', weights.astype(jnp.float32), value_blocks)
    overall = lax.optimization_barrier(jnp.max(block_max, axis=0))
    factor = jnp.exp(block_max - overall[None])
    total_sum = lax.optimization_barrier(jnp.sum(factor * block_total, axis=0))
    weighted = lax.optimization_barrier(jnp.sum(factor[..., None] * block_out, axis=0))
    return (weighted / total_sum[..., None]).astype(jnp.bfloat16)

def one_request(inputs):
    length, page_rows, queries, new_keys, new_values, key_cache, value_cache = inputs
    positions = length + jnp.arange(C, dtype=jnp.int32)
    query_heads = rotate(queries.reshape(C, HEADS, HD).astype(jnp.float32).transpose(1, 0, 2), positions).astype(jnp.bfloat16)
    key_heads = rotate(new_keys.reshape(C, KVH, HD).astype(jnp.float32).transpose(1, 0, 2), positions).astype(jnp.bfloat16)
    value_heads = new_values.reshape(C, KVH, HD).transpose(1, 0, 2)
    page_ids = jnp.arange(NPAGE, dtype=jnp.int32)
    logical = lax.optimization_barrier(jnp.sum(jnp.where(page_rows[None, :] == page_ids[:, None], page_ids[None, :], 0), axis=1))
    slot_position = (logical[:, None] * PAGE + jnp.arange(PAGE, dtype=jnp.int32)[None, :]).reshape(NPAGE * PAGE)
    new_index = slot_position - length
    is_new = (new_index >= 0) & (new_index < C)
    chosen = jnp.clip(new_index, 0, C - 1)
    key_flat = jnp.where(is_new[None, :, None], key_heads[:, chosen], key_cache.reshape(KVH, NPAGE * PAGE, HD))
    value_flat = jnp.where(is_new[None, :, None], value_heads[:, chosen], value_cache.reshape(KVH, NPAGE * PAGE, HD))
    attn = lax.map(lambda group_in: attend_head(group_in[0], group_in[1], group_in[2], slot_position, positions), (query_heads.reshape(KVH, GROUP, C, HD), key_flat, value_flat))
    attn_rows = attn.reshape(HEADS, C, HD).transpose(1, 0, 2).reshape(C, HEADS * HD)
    return (attn_rows, key_flat.reshape(KVH, NPAGE, PAGE, HD), value_flat.reshape(KVH, NPAGE, PAGE, HD))

def reference(x_resid, q_new, k_new, v_new, k_cache, v_cache, cache_len, page_table, wo, norm_gain, w_gate, w_up, w_down):
    attn, key_out, value_out = lax.map(one_request, (cache_len, page_table, q_new, k_new, v_new, k_cache, v_cache))

    def feed_forward(inputs):
        residual_in, attn_rows = inputs
        resid = residual_in.astype(jnp.float32) + jnp.dot(attn_rows, wo, preferred_element_type=jnp.float32)
        normed = (resid * lax.rsqrt(lax.optimization_barrier(jnp.mean(resid * resid, axis=-1, keepdims=True)) + 1e-05) * norm_gain.astype(jnp.float32)).astype(jnp.bfloat16)
        gate_val = jnp.dot(normed, w_gate, preferred_element_type=jnp.float32)
        up_val = jnp.dot(normed, w_up, preferred_element_type=jnp.float32)
        hidden = (jax.nn.silu(gate_val) * up_val).astype(jnp.bfloat16)
        return (resid + jnp.dot(hidden, w_down, preferred_element_type=jnp.float32)).astype(jnp.bfloat16)
    layer_out = lax.map(feed_forward, (x_resid, attn))
    return (layer_out, key_out, value_out)
```

```python
import functools
import math

import jax
import jax.numpy as jnp
from jax import lax
from jax.experimental import pallas as pl
from jax.experimental.pallas import tpu as pltpu
from jax.sharding import PartitionSpec as P

MESH = pl.DeviceIdType.MESH
SIDE = 4
RING = 8
ROWS = 16
BF16, F32 = jnp.bfloat16, jnp.float32


def torus_plan():
    entries, got = [], {}

    def add(rnd, offset, first, count, direction):
        need = sorted({got[offset, q] for q in range(first, first + count)}) if offset != (0, 0) else []
        there = tuple((o - d) % SIDE for o, d in zip(offset, direction))
        for q in range(first, first + count):
            assert (there, q) not in got and there != (0, 0)
            got[there, q] = len(entries)
        entries.append((rnd, offset, first, count, direction, need))

    east, west, north, south = (1, 0), (-1, 0), (0, 1), (0, -1)
    for direction in (east, west, north, south):
        add(0, (0, 0), 0, 4, direction)
    for offset, half, quarters, ahead, across in (
        ((1, 0), 0, (0, 2), west, (north, south)),
        ((3, 0), 0, (1, 3), east, (north, south)),
        ((0, 1), 2, (0, 2), south, (east, west)),
        ((0, 3), 2, (1, 3), north, (east, west)),
    ):
        for direction in across:
            add(1, offset, half, 2, direction)
        for quarter in quarters:
            add(1, offset, quarter, 1, ahead)
    for direction in (north, south):
        add(2, (2, 0), 0, 2, direction)
    for direction in (east, west):
        add(2, (0, 2), 2, 2, direction)
    for offset in ((1, 1), (3, 1), (1, 3), (3, 3)):
        add(2, offset, *((0, 1, south) if offset[1] == 1 else (1, 1, north)))
        add(2, offset, *((2, 1, west) if offset[0] == 1 else (3, 1, east)))
    add(3, (2, 1), 0, 1, south)
    add(3, (2, 3), 1, 1, north)
    add(3, (1, 2), 2, 1, west)
    add(3, (3, 2), 3, 1, east)
    assert len(got) == 4 * (SIDE * SIDE - 1)
    return entries


PLAN = torus_plan()
STREAMS = ((1, 0, 4), (-1, 1, 4), (-1, 0, 3), (1, 1, 3))
BASE = (0, 4, 8, 11)
SLOTS_Z = 14


def kernel(
    q_ref, rel_ref, x_ref, gain_ref, k_hbm, v_hbm, wo_hbm, gu_hbm, dt_hbm,
    out_ref,
    k_vm, v_vm, wo_vm, gu_vm, dt_vm, mine, theirs, sent, attn, pb, nb, acc, hid, resid,
    snd, rcv, snd2, rcv2, xs, xr,
    local_sem, gu_s, gu_r, dt_s, dt_r, one_s, one_r, z1_s, z1_r, zg_s, zg_r, z2_s, z2_r, chip_s, chip_r, ex_s, ex_r,
):
    req, kz, core = lax.axis_index("req"), lax.axis_index("kv"), lax.axis_index("blk")
    other = 1 - core
    mx, my = lax.rem(req, SIDE), lax.div(req, SIDE)
    width = pb.shape[2]
    half = width // 2
    quarter = width // 4
    heads = q_ref.shape[1]
    half_tokens = q_ref.shape[2]
    head_dim = q_ref.shape[3]
    partner = (req, kz, other)

    def plane(offset):
        x = lax.rem(mx + (offset[0] % SIDE), SIDE)
        y = lax.rem(my + (offset[1] % SIDE), SIDE)
        return y * SIDE + x

    def ring(step):
        return lax.rem(kz + (step % RING), RING)

    pending = []

    def send(src, dst, ssem, rsem, device):
        copy = pltpu.make_async_remote_copy(
            src_ref=src, dst_ref=dst, send_sem=ssem, recv_sem=rsem, device_id=device, device_id_type=MESH
        )
        copy.start()
        pending.append(copy)

    def arrive(dst, ssem, rsem, device):
        pltpu.make_async_remote_copy(
            src_ref=dst, dst_ref=dst, send_sem=ssem, recv_sem=rsem, device_id=device, device_id_type=MESH
        ).wait_recv()

    shard = gu_hbm.shape[0]
    part = shard // 4
    own_rows = pl.ds(pl.multiple_of(req * shard, 16), shard)
    wo_rows = wo_hbm.shape[0]
    local = [
        pltpu.make_async_copy(k_hbm, k_vm, local_sem.at[0]),
        pltpu.make_async_copy(v_hbm, v_vm, local_sem.at[1]),
        pltpu.make_async_copy(gu_hbm, gu_vm.at[own_rows], local_sem.at[2]),
        pltpu.make_async_copy(dt_hbm, dt_vm.at[own_rows], local_sem.at[3]),
        pltpu.make_async_copy(
            wo_hbm, wo_vm.at[pl.ds(pl.multiple_of(core * wo_rows, 16), wo_rows)], local_sem.at[4]
        ),
    ]
    for copy in local:
        copy.start()
    barrier = pltpu.get_barrier_semaphore()
    friends = [(plane(d), kz, core) for d in ((1, 0), (-1, 0), (0, 1), (0, -1))]
    friends += [(req, ring(1), core), (req, ring(-1), core), partner]
    for friend in friends:
        pl.semaphore_signal(barrier, inc=1, device_id=friend, device_id_type=MESH)
    pl.semaphore_wait(barrier, len(friends))

    stream = {"gu": (gu_hbm, gu_vm, gu_s, gu_r), "dt": (dt_hbm, dt_vm, dt_s, dt_r)}
    landed = {"gu": set(), "dt": set()}

    def rows_of(offset, first, count):
        start = plane(offset) * shard + first * part
        return pl.ds(pl.multiple_of(start, 16), count * part)

    def land(name, index):
        if index in landed[name]:
            return
        landed[name].add(index)
        _, full, ssem, rsem = stream[name]
        _, offset, first, count, direction, _ = PLAN[index]
        here = tuple((o - d) % SIDE for o, d in zip(offset, direction))
        back = tuple(-d for d in direction)
        arrive(full.at[rows_of(here, first, count)], ssem.at[index], rsem.at[index], (plane(back), kz, core))

    def issue(name, rnd):
        source, full, ssem, rsem = stream[name]
        for index, (when, offset, first, count, direction, need) in enumerate(PLAN):
            if when != rnd:
                continue
            for earlier in need:
                land(name, earlier)
            rows = rows_of(offset, first, count)
            src = source if offset == (0, 0) else full.at[rows]
            send(src, full.at[rows], ssem.at[index], rsem.at[index], (plane(direction), kz, core))

    issue("gu", 0)
    own_wo = wo_vm.at[pl.ds(pl.multiple_of(core * wo_rows, 16), wo_rows)]
    send(wo_hbm, own_wo, one_s.at[0], one_r.at[0], partner)
    issue("dt", 0)

    scale = 1.0 / math.sqrt(head_dim)
    local[0].wait()
    local[1].wait()

    def attend(part_id, result):
        row = lax.broadcasted_iota(jnp.int32, (half_tokens, 1), 0)
        token = (row // ROWS) * (2 * ROWS) + row % ROWS + part_id * ROWS
        lane = lax.broadcasted_iota(jnp.int32, (half_tokens, head_dim), 1)

        def head(g, carry):
            score = lax.dot_general(
                q_ref[part_id, g], k_vm[...], (((1,), (1,)), ((), ())), preferred_element_type=F32
            )
            allowed = rel_ref[...] <= token
            score = jnp.where(allowed, score * scale, -1e30)
            top = jnp.max(score, axis=-1, keepdims=True)
            weight = jnp.where(allowed, jnp.exp(score - top), 0.0)
            total = jnp.sum(weight, axis=-1, keepdims=True)
            result[g, :, :head_dim] = jnp.dot(weight.astype(BF16), v_vm[...], preferred_element_type=F32)
            result[g, :, head_dim:] = jnp.where(lane < head_dim // 2, top, total)
            return carry

        lax.fori_loop(0, heads, head, 0)

    attend(other, sent)
    send(sent, theirs, one_s.at[1], one_r.at[1], partner)
    attend(core, mine)
    arrive(theirs, one_s.at[1], one_r.at[1], partner)
    mid = head_dim + head_dim // 2
    for g in range(heads):
        a, b = mine[g], theirs[g]
        top_a, top_b = a[:, head_dim : head_dim + 1], b[:, head_dim : head_dim + 1]
        top = jnp.maximum(top_a, top_b)
        fa, fb = jnp.exp(top_a - top), jnp.exp(top_b - top)
        total = fa * a[:, mid : mid + 1] + fb * b[:, mid : mid + 1]
        value = (fa * a[:, :head_dim] + fb * b[:, :head_dim]) / total
        attn[:, g * head_dim : (g + 1) * head_dim] = value.astype(BF16)

    def columns(part_id):
        return slice(part_id * half, (part_id + 1) * half)

    def ring_send(s, j, out_buf, in_buf, ssem, rsem):
        direction, part_id, reach = STREAMS[s]
        slot = BASE[s] + j
        value = pb[ring(direction * (reach - j)), :, columns(part_id)]
        if j > 0:
            arrive(in_buf.at[slot - 1], ssem.at[slot - 1], rsem.at[slot - 1], (req, ring(-direction), core))
            value = value + in_buf[slot - 1].astype(F32)
        out_buf[slot] = value.astype(BF16)
        send(out_buf.at[slot], in_buf.at[slot], ssem.at[slot], rsem.at[slot], (req, ring(direction), core))

    def ring_total(part_id, in_buf, ssem, rsem):
        value = pb[kz, :, columns(part_id)]
        for s, (direction, p, reach) in enumerate(STREAMS):
            if p == part_id:
                slot = BASE[s] + reach - 1
                arrive(in_buf.at[slot], ssem.at[slot], rsem.at[slot], (req, ring(-direction), core))
                value = value + in_buf[slot].astype(F32)
        return value

    local[4].wait()
    theirs_wo = wo_vm.at[pl.ds(pl.multiple_of(other * wo_rows, 16), wo_rows)]
    arrive(theirs_wo, one_s.at[0], one_r.at[0], partner)
    for c in range(4):
        cols = slice(c * quarter, (c + 1) * quarter)
        block = jnp.dot(attn[...], wo_vm[:, cols], preferred_element_type=F32)
        pb[:, :, cols] = block.reshape(RING, ROWS, quarter)
        if c % 2 == 1:
            for s in range(4):
                if STREAMS[s][1] == c // 2:
                    ring_send(s, 0, snd, rcv, z1_s, z1_r)
    issue("gu", 1)
    for j in range(1, 4):
        for s in range(4):
            if j < STREAMS[s][2]:
                ring_send(s, j, snd, rcv, z1_s, z1_r)
    for p in range(2):
        resid[:, columns(p)] = ring_total(p, rcv, z1_s, z1_r) + x_ref[:, columns(p)].astype(F32)
    rows = resid[...]
    inverse = lax.rsqrt(jnp.mean(rows * rows, axis=-1, keepdims=True) + 1e-05)
    nb[kz] = (rows * inverse * gain_ref[...].astype(F32)).astype(BF16)

    def chip_send(step, part_id):
        slot = part_id * RING + step % RING
        block = ring(step)
        send(
            nb.at[block, :, columns(part_id)], nb.at[RING + block, :, columns(part_id)],
            chip_s.at[slot], chip_r.at[slot], partner,
        )

    def gather_arrive(s, j):
        direction, part_id, _ = STREAMS[s]
        slot = BASE[s] + j
        step = -direction * (j + 1)
        arrive(nb.at[ring(step), :, columns(part_id)], zg_s.at[slot], zg_r.at[slot], (req, ring(-direction), core))

    def gather_send(s, j):
        direction, part_id, _ = STREAMS[s]
        slot = BASE[s] + j
        block = nb.at[ring(-direction * j), :, columns(part_id)]
        send(block, block, zg_s.at[slot], zg_r.at[slot], (req, ring(direction), core))

    order = (0, 2, 1, 3)
    for s in order:
        gather_send(s, 0)
    for p in range(2):
        chip_send(0, p)
    for j in range(1, 4):
        for s in order:
            direction, part_id, reach = STREAMS[s]
            gather_arrive(s, j - 1)
            if j < reach:
                gather_send(s, j)
            chip_send(-direction * j, part_id)
        if j == 1:
            issue("gu", 2)
            issue("dt", 1)
    for s in (0, 1):
        direction, part_id, reach = STREAMS[s]
        gather_arrive(s, reach - 1)
        chip_send(-direction * reach, part_id)
    issue("gu", 3)
    local[2].wait()
    for index in range(len(PLAN)):
        land("gu", index)

    for c in range(4):
        if c % 2 == 0:
            for step in range(RING):
                slot = (c // 2) * RING + step
                block = nb.at[RING + ring(step), :, columns(c // 2)]
                arrive(block, chip_s.at[slot], chip_r.at[slot], partner)
        cols = slice(c * quarter, (c + 1) * quarter)
        value = jnp.dot(
            nb[:, :, cols].reshape(2 * RING * ROWS, quarter), gu_vm[cols, :], preferred_element_type=F32
        )
        if c == 0:
            acc[...] = value
        else:
            acc[...] += value
    units = hid.shape[1]
    whole = units // 128 * 128
    gate, up = acc[:, :whole], acc[:, whole + 128 :]
    hid[:, :whole] = (gate / (1.0 + jnp.exp(-gate)) * up).astype(BF16)
    gate = acc[:, whole : whole + 128]
    up = pltpu.roll(gate, 64, 1)
    tail = (gate / (1.0 + jnp.exp(-gate)) * up).astype(BF16)
    hid[:, whole:] = tail[:, : units - whole]

    issue("dt", 2)
    issue("dt", 3)
    local[3].wait()
    for index in range(len(PLAN)):
        land("dt", index)
    for c in range(4):
        cols = slice(c * quarter, (c + 1) * quarter)
        value = lax.dot_general(hid[...], dt_vm[cols, :], (((1,), (1,)), ((), ())), preferred_element_type=F32)
        pb[:, :, cols] = value[: RING * ROWS].reshape(RING, ROWS, quarter)
        xs[:, :, cols] = value[RING * ROWS :].astype(BF16).reshape(RING, ROWS, quarter)
        send(xs.at[:, :, cols], xr.at[:, :, cols], ex_s.at[c], ex_r.at[c], partner)
    for c in range(4):
        cols = slice(c * quarter, (c + 1) * quarter)
        arrive(xr.at[:, :, cols], ex_s.at[c], ex_r.at[c], partner)
        pb[:, :, cols] += xr[:, :, cols].astype(F32)
        if c % 2 == 1:
            for s in range(4):
                if STREAMS[s][1] == c // 2:
                    ring_send(s, 0, snd2, rcv2, z2_s, z2_r)
    for j in range(1, 4):
        for s in range(4):
            if j < STREAMS[s][2]:
                ring_send(s, j, snd2, rcv2, z2_s, z2_r)
    for p in range(2):
        out_ref[:, columns(p)] = (resid[:, columns(p)] + ring_total(p, rcv2, z2_s, z2_r)).astype(BF16)
    for copy in pending:
        copy.wait_send()


def layer(q, rel, x, gain, keys, values, wo, gate_up, down):
    width = x.shape[1]
    hidden = down.shape[1]
    slots = keys.shape[0]
    head_dim = keys.shape[1]
    heads, half_tokens = q.shape[1], q.shape[2]
    vmem = pl.BlockSpec(memory_space=pltpu.VMEM)
    hbm = pl.BlockSpec(memory_space=pl.ANY)
    dma = pltpu.SemaphoreType.DMA
    part = pltpu.VMEM((heads, half_tokens, 2 * head_dim), F32)
    hop = pltpu.VMEM((SLOTS_Z, ROWS, width // 2), BF16)
    plan = dma((len(PLAN),))
    return pl.pallas_call(
        kernel,
        out_shape=jax.ShapeDtypeStruct(x.shape, BF16),
        in_specs=[vmem] * 4 + [hbm] * 5,
        out_specs=vmem,
        scratch_shapes=[
            pltpu.VMEM((slots, head_dim), BF16),
            pltpu.VMEM((slots, head_dim), BF16),
            pltpu.VMEM((2 * wo.shape[0], width), BF16),
            pltpu.VMEM((width, gate_up.shape[1]), BF16),
            pltpu.VMEM((width, hidden), BF16),
            part, part, part,
            pltpu.VMEM((half_tokens, heads * head_dim), BF16),
            pltpu.VMEM((RING, ROWS, width), F32),
            pltpu.VMEM((2 * RING, ROWS, width), BF16),
            pltpu.VMEM((2 * RING * ROWS, gate_up.shape[1]), F32),
            pltpu.VMEM((2 * RING * ROWS, hidden), BF16),
            pltpu.VMEM((ROWS, width), F32),
            hop, hop, hop, hop,
            pltpu.VMEM((RING, ROWS, width), BF16),
            pltpu.VMEM((RING, ROWS, width), BF16),
            dma((5,)),
            plan, plan, plan, plan,
            dma((2,)), dma((2,)),
            dma((SLOTS_Z,)), dma((SLOTS_Z,)), dma((SLOTS_Z,)), dma((SLOTS_Z,)), dma((SLOTS_Z,)), dma((SLOTS_Z,)),
            dma((2 * RING,)), dma((2 * RING,)),
            dma((4,)), dma((4,)),
        ],
        compiler_params=pltpu.CompilerParams(
            collective_id=0, has_side_effects=True, vmem_limit_bytes=62 * 2**20
        ),
        name="layer",
    )(q, rel, x, gain, keys, values, wo, gate_up, down)


def rotate(field, positions):
    half_width = field.shape[-1] // 2
    pair_index = jnp.arange(half_width, dtype=F32)
    frequency = jnp.power(1000000.0, -2.0 * pair_index / field.shape[-1])
    angles = positions.astype(F32)[:, None] * frequency[None, :]
    cosine, sine = jnp.cos(angles)[:, None, :], jnp.sin(angles)[:, None, :]
    lower, upper = field[..., :half_width], field[..., half_width:]
    return jnp.concatenate([lower * cosine - upper * sine, upper * cosine + lower * sine], axis=-1)


def on_device(
    x_resid, q_new, k_new, v_new, k_cache, v_cache, cache_len, page_table, wo, norm_gain, w_gate, w_up, w_down
):
    blk_id = lax.axis_index("blk")
    new_tokens, head_dim = k_new.shape[1:]
    group = q_new.shape[2] // head_dim
    slot_count, page_size = k_cache.shape[2:4]
    page_total = page_table.shape[1]
    length = cache_len[0]
    positions = length + jnp.arange(new_tokens, dtype=jnp.int32)
    both = jnp.concatenate(
        [q_new[0].reshape(new_tokens, group, head_dim), k_new[0].reshape(new_tokens, 1, head_dim)], axis=1
    )
    turned = rotate(both.astype(F32), positions).astype(BF16)
    queries = turned[:, :group].reshape(RING, 2, ROWS, group, head_dim).transpose(1, 3, 0, 2, 4)
    queries = queries.reshape(2, group, new_tokens // 2, head_dim)

    first_page, shift = length // page_size, length % page_size
    images = 3
    fresh = jnp.concatenate([turned[:, group], v_new[0]], axis=1)
    place = jnp.arange(images * page_size, dtype=jnp.int32)[:, None]
    source = jnp.arange(new_tokens, dtype=jnp.int32)[None, :]
    moved = jnp.dot((place == source + shift).astype(BF16), fresh, preferred_element_type=F32).astype(BF16)
    moved = moved.reshape(images, page_size, 2 * head_dim)
    page_ids = jnp.arange(page_total, dtype=jnp.int32)
    physical = blk_id * slot_count + jnp.arange(slot_count, dtype=jnp.int32)
    logical = jnp.sum(jnp.where(page_table[0][None, :] == physical[:, None], page_ids[None, :], 0), axis=1)
    new_index = logical[:, None] * page_size + jnp.arange(page_size, dtype=jnp.int32)[None, :] - length
    is_new = ((new_index >= 0) & (new_index < new_tokens))[:, :, None]
    which = (logical - first_page)[:, None, None]

    def written(cache, columns):
        image = moved[:, :, columns]
        picked = jnp.where(which == 0, image[0], jnp.where(which == 1, image[1], image[2]))
        return jnp.where(is_new, picked, cache[0, 0])

    keys = written(k_cache, slice(0, head_dim))
    values = written(v_cache, slice(head_dim, 2 * head_dim))
    whole = w_gate.shape[1] // 128 * 128
    gate_up = jnp.concatenate([w_gate, w_up[:, whole:], w_up[:, :whole]], axis=1)
    layer_out = layer(
        queries,
        new_index.reshape(1, slot_count * page_size),
        x_resid[0],
        norm_gain[None],
        keys.reshape(slot_count * page_size, head_dim),
        values.reshape(slot_count * page_size, head_dim),
        wo,
        gate_up,
        w_down.T,
    )
    return (layer_out[None], keys[None, None], values[None, None])


def solution(mesh):
    in_specs = (
        P("req", ("kv", "blk"), None),
        P("req", None, "kv"),
        P("req", None, "kv"),
        P("req", None, "kv"),
        P("req", "kv", "blk", None, None),
        P("req", "kv", "blk", None, None),
        P("req"),
        P("req", None),
        P(("kv", "blk"), None),
        P(),
        P("req", ("kv", "blk")),
        P("req", ("kv", "blk")),
        P(("kv", "blk"), "req"),
    )
    out_specs = (
        P("req", ("kv", "blk"), None),
        P("req", "kv", "blk", None, None),
        P("req", "kv", "blk", None, None),
    )
    return jax.shard_map(on_device, mesh=mesh, in_specs=in_specs, out_specs=out_specs, check_vma=False)
```

```python
import functools
import math

import jax
import jax.numpy as jnp
from jax import lax
from jax.experimental import pallas as pl
from jax.experimental.pallas import tpu as pltpu
from jax.sharding import PartitionSpec as P

MESH = pl.DeviceIdType.MESH
SIDE = 4
RING = 8
ROWS = 16
BF16, F32 = jnp.bfloat16, jnp.float32


def torus_plan():
    entries, got = [], {}

    def add(rnd, offset, first, count, direction):
        need = sorted({got[offset, q] for q in range(first, first + count)}) if offset != (0, 0) else []
        there = tuple((o - d) % SIDE for o, d in zip(offset, direction))
        for q in range(first, first + count):
            assert (there, q) not in got and there != (0, 0)
            got[there, q] = len(entries)
        entries.append((rnd, offset, first, count, direction, need))

    east, west, north, south = (1, 0), (-1, 0), (0, 1), (0, -1)
    for direction in (east, west, north, south):
        add(0, (0, 0), 0, 4, direction)
    late = []
    for offset, half, quarters, ahead, across in (
        ((1, 0), 0, (0, 2), west, (north, south)),
        ((3, 0), 0, (1, 3), east, (north, south)),
        ((0, 1), 2, (0, 2), south, (east, west)),
        ((0, 3), 2, (1, 3), north, (east, west)),
    ):
        for quarter in quarters:
            add(1, offset, quarter, 1, ahead)
        for direction in across:
            late.append((1, offset, half, 2, direction))
    for entry in late:
        add(*entry)
    for direction in (north, south):
        add(2, (2, 0), 0, 2, direction)
    for direction in (east, west):
        add(2, (0, 2), 2, 2, direction)
    for offset in ((1, 1), (3, 1), (1, 3), (3, 3)):
        add(2, offset, *((0, 1, south) if offset[1] == 1 else (1, 1, north)))
        add(2, offset, *((2, 1, west) if offset[0] == 1 else (3, 1, east)))
    add(3, (2, 1), 0, 1, south)
    add(3, (2, 3), 1, 1, north)
    add(3, (1, 2), 2, 1, west)
    add(3, (3, 2), 3, 1, east)
    assert len(got) == 4 * (SIDE * SIDE - 1)
    return entries


PLAN = torus_plan()
STREAMS = ((1, 0, 4), (-1, 1, 4), (-1, 0, 3), (1, 1, 3))
BASE = (0, 4, 8, 11)
SLOTS_Z = 14
PLACES = (
    (0, 0), (1, 0), (3, 0), (0, 1), (0, 3), (2, 0), (0, 2), (1, 1), (3, 1), (1, 3),
    (3, 3), (2, 1), (2, 3), (1, 2), (3, 2), (2, 2),
)
EARLY = 10


def kernel(
    q_ref, fresh_k, fresh_v, cos_ref, sin_ref, len_ref, table_ref, x_ref, gain_ref,
    k_hbm, v_hbm, wo_hbm, gate_hbm, up_hbm, dn_hbm,
    out_ref, resid, k_out, v_out,
    q_vm, image, logic, rel_ref, k_vm, v_vm, wo_vm, gate_vm, up_vm, gu_vm, dn_vm, raw, gain_row, dt_vm, mine, theirs, sent, attn, pb, nb, acc, hid,
    snd, rcv, snd2, rcv2, snd3, rcv3, xs, xr,
    local_sem, gu_s, gu_r, dt_s, dt_r, one_s, one_r, z1_s, z1_r, zg_s, zg_r, z2_s, z2_r, z3_s, z3_r,
    chip_s, chip_r, ex_s, ex_r,
):
    req, kz, core = lax.axis_index("req"), lax.axis_index("kv"), lax.axis_index("blk")
    other = 1 - core
    mx, my = lax.rem(req, SIDE), lax.div(req, SIDE)
    width = pb.shape[2]
    half = width // 2
    quarter = width // 4
    heads, half_tokens, head_dim = q_vm.shape[1:]
    tokens = 2 * half_tokens
    partner = (req, kz, other)

    def plane(offset):
        x = lax.rem(mx + (offset[0] % SIDE), SIDE)
        y = lax.rem(my + (offset[1] % SIDE), SIDE)
        return y * SIDE + x

    def ring(step):
        return lax.rem(kz + (step % RING), RING)

    pending = []

    def send(src, dst, ssem, rsem, device):
        copy = pltpu.make_async_remote_copy(
            src_ref=src, dst_ref=dst, send_sem=ssem, recv_sem=rsem, device_id=device, device_id_type=MESH
        )
        copy.start()
        pending.append(copy)

    def arrive(dst, ssem, rsem, device):
        pltpu.make_async_remote_copy(
            src_ref=dst, dst_ref=dst, send_sem=ssem, recv_sem=rsem, device_id=device, device_id_type=MESH
        ).wait_recv()

    shard, units = gate_hbm.shape
    whole = units // 128 * 128
    part = shard // 4
    own_rows = pl.ds(pl.multiple_of(req * shard, 16), shard)
    wo_rows = wo_hbm.shape[0]
    local = [
        pltpu.make_async_copy(k_hbm, k_vm, local_sem.at[0]),
        pltpu.make_async_copy(v_hbm, v_vm, local_sem.at[1]),
        pltpu.make_async_copy(gate_hbm, gate_vm, local_sem.at[2]),
        pltpu.make_async_copy(dn_hbm, dn_vm, local_sem.at[3]),
        pltpu.make_async_copy(
            wo_hbm, wo_vm.at[pl.ds(pl.multiple_of(core * wo_rows, 16), wo_rows)], local_sem.at[4]
        ),
        pltpu.make_async_copy(up_hbm, up_vm, local_sem.at[7]),
    ]
    for n in (2, 5, 0, 1, 3, 4):
        local[n].start()
    barrier = pltpu.get_barrier_semaphore()
    friends = [(plane(d), kz, core) for d in ((1, 0), (-1, 0), (0, 1), (0, -1))]
    friends += [(req, ring(1), core), (req, ring(-1), core), partner]
    for friend in friends:
        pl.semaphore_signal(barrier, inc=1, device_id=friend, device_id_type=MESH)
    pl.semaphore_wait(barrier, len(friends))

    stream = {"gu": (gu_vm, gu_s, gu_r), "dt": (raw, dt_s, dt_r)}
    packed = raw.shape[0] // (SIDE * SIDE)
    tiles = packed // 16
    cuts = [16 * ((tiles * q + 3) // 4) for q in range(5)]
    landed = {"gu": set(), "dt": set()}

    def rows_of(name, offset, first, count):
        offset = tuple(o % SIDE for o in offset)
        if name == "dt":
            return pl.ds(PLACES.index(offset) * packed + cuts[first], cuts[first + count] - cuts[first])
        return pl.ds(pl.multiple_of(plane(offset) * shard + first * part, 16), count * part)

    def land(name, index):
        if index in landed[name]:
            return
        landed[name].add(index)
        full, ssem, rsem = stream[name]
        _, offset, first, count, direction, _ = PLAN[index]
        here = tuple(o - d for o, d in zip(offset, direction))
        back = tuple(-d for d in direction)
        arrive(full.at[rows_of(name, here, first, count)], ssem.at[index], rsem.at[index], (plane(back), kz, core))

    def issue(name, rnd):
        full, ssem, rsem = stream[name]
        for index, (when, offset, first, count, direction, need) in enumerate(PLAN):
            if when != rnd:
                continue
            for earlier in need:
                land(name, earlier)
            there = offset if name == "gu" else tuple(o - d for o, d in zip(offset, direction))
            src = full.at[rows_of(name, offset, first, count)]
            dst = full.at[rows_of(name, there, first, count)]
            send(src, dst, ssem.at[index], rsem.at[index], (plane(direction), kz, core))

    local[2].wait()
    local[5].wait()
    gu_vm[own_rows, :whole] = gate_vm[:, :whole]
    gu_vm[own_rows, whole : whole + 128] = jnp.concatenate([gate_vm[:, whole:], up_vm[:, whole:]], axis=1)
    gu_vm[own_rows, whole + 128 :] = up_vm[:, :whole]
    issue("gu", 0)
    own_wo = wo_vm.at[pl.ds(pl.multiple_of(core * wo_rows, 16), wo_rows)]
    send(wo_hbm, own_wo, one_s.at[0], one_r.at[0], partner)

    cosine = jnp.concatenate([cos_ref[...], cos_ref[...]], axis=1)
    sine = jnp.concatenate([-sin_ref[...], sin_ref[...]], axis=1)

    def turn(rows):
        return rows * cosine + pltpu.roll(rows, head_dim // 2, 1) * sine

    for g in range(heads):
        turned = turn(q_ref[:, g * head_dim : (g + 1) * head_dim].astype(F32)).astype(BF16)
        turned = turned.reshape(RING, 2, ROWS, head_dim)
        for p in range(2):
            q_vm[p, g] = turned[:, p].reshape(half_tokens, head_dim)

    page = 128
    pages = logic.shape[0]
    table_len = table_ref.shape[1]
    length = len_ref[...].astype(F32)
    first_page = jnp.floor(length * (1.0 / page))
    shift = length - first_page * page
    place = lax.broadcasted_iota(jnp.int32, (3 * page, tokens), 0) - lax.broadcasted_iota(
        jnp.int32, (3 * page, tokens), 1
    )
    chosen = jnp.where(place.astype(F32) == shift, 1.0, 0.0).astype(BF16)
    image[:, :head_dim] = jnp.dot(chosen, turn(fresh_k[...].astype(F32)).astype(BF16), preferred_element_type=F32)
    image[:, head_dim:] = jnp.dot(chosen, fresh_v[...], preferred_element_type=F32)
    physical = lax.broadcasted_iota(jnp.int32, (pages, table_len), 0) + core * pages
    ids = lax.broadcasted_iota(jnp.int32, (pages, table_len), 1).astype(F32)
    held = jnp.sum(jnp.where(table_ref[...] == physical, ids, 0.0), axis=1, keepdims=True)
    logic[...] = jnp.broadcast_to(held, logic.shape)
    lanes = lax.broadcasted_iota(jnp.int32, (1, page), 1).astype(F32)
    for s in range(pages):
        rel_ref[:, s * page : (s + 1) * page] = logic[s : s + 1, :] * page - length + lanes
    local[0].wait()
    local[1].wait()
    down_rows = lax.broadcasted_iota(jnp.int32, (page, page), 0).astype(F32)

    def write(s, carry):
        number = logic[pl.ds(s, 1), :]
        index = down_rows + (number * page - length)
        new = (index >= 0.0) & (index < float(tokens))
        which = jnp.broadcast_to(number - first_page, (page, page))
        at = pl.ds(pl.multiple_of(s * page, page), page)
        for cache, low in ((k_vm, 0), (v_vm, head_dim)):
            a, b, c = (image[n * page : (n + 1) * page, low : low + head_dim] for n in range(3))
            picked = jnp.where(which == 0.0, a, jnp.where(which == 1.0, b, c))
            cache[at, :] = jnp.where(new, picked, cache[at, :].astype(F32)).astype(BF16)
        return carry

    lax.fori_loop(0, pages, write, 0)
    saved = [
        pltpu.make_async_copy(k_vm, k_out, local_sem.at[5]),
        pltpu.make_async_copy(v_vm, v_out, local_sem.at[6]),
    ]
    for copy in saved:
        copy.start()

    scale = 1.0 / math.sqrt(head_dim)

    def attend(part_id, result):
        row = lax.broadcasted_iota(jnp.int32, (half_tokens, 1), 0)
        token = ((row // ROWS) * (2 * ROWS) + row % ROWS + part_id * ROWS).astype(F32)
        lane = lax.broadcasted_iota(jnp.int32, (half_tokens, head_dim), 1)

        def head(g, carry):
            score = lax.dot_general(
                q_vm[part_id, g], k_vm[...], (((1,), (1,)), ((), ())), preferred_element_type=F32
            )
            allowed = rel_ref[...] <= token
            score = jnp.where(allowed, score * scale, -1e30)
            top = jnp.max(score, axis=-1, keepdims=True)
            weight = jnp.where(allowed, jnp.exp(score - top), 0.0)
            total = jnp.sum(weight, axis=-1, keepdims=True)
            result[g, :, :head_dim] = jnp.dot(weight.astype(BF16), v_vm[...], preferred_element_type=F32)
            result[g, :, head_dim:] = jnp.where(lane < head_dim // 2, top, total)
            return carry

        lax.fori_loop(0, heads, head, 0)

    attend(other, sent)
    send(sent, theirs, one_s.at[1], one_r.at[1], partner)

    fold = shard // 2
    local[3].wait()
    for n in range(whole // 128):
        raw[n * shard : (n + 1) * shard] = dn_vm[:, n * 128 : (n + 1) * 128]
    raw[packed - fold : packed] = jnp.concatenate([dn_vm[:fold, whole:], dn_vm[fold:, whole:]], axis=1)
    issue("dt", 0)
    attend(core, mine)
    arrive(theirs, one_s.at[1], one_r.at[1], partner)
    mid = head_dim + head_dim // 2
    for g in range(heads):
        a, b = mine[g], theirs[g]
        top_a, top_b = a[:, head_dim : head_dim + 1], b[:, head_dim : head_dim + 1]
        top = jnp.maximum(top_a, top_b)
        fa, fb = jnp.exp(top_a - top), jnp.exp(top_b - top)
        total = fa * a[:, mid : mid + 1] + fb * b[:, mid : mid + 1]
        value = (fa * a[:, :head_dim] + fb * b[:, :head_dim]) / total
        attn[:, g * head_dim : (g + 1) * head_dim] = value.astype(BF16)

    def columns(part_id):
        return slice(part_id * half, (part_id + 1) * half)

    def ring_send(s, j, spans, out_buf, in_buf, ssem, rsem):
        direction, part_id, reach = STREAMS[s]
        start, size = spans[part_id]
        slot = BASE[s] + j
        value = pb[ring(direction * (reach - j)), :, start : start + size]
        if j > 0:
            ring_arrive(s, j - 1, size, in_buf, ssem, rsem)
            value = value + in_buf[slot - 1, :, :size].astype(F32)
        out_buf[slot, :, :size] = value.astype(BF16)
        here, there = out_buf.at[slot, :, :size], in_buf.at[slot, :, :size]
        send(here, there, ssem.at[slot], rsem.at[slot], (req, ring(direction), core))

    def ring_arrive(s, j, size, in_buf, ssem, rsem):
        slot = BASE[s] + j
        there = in_buf.at[slot, :, :size]
        arrive(there, ssem.at[slot], rsem.at[slot], (req, ring(-STREAMS[s][0]), core))

    def ring_total(part_id, spans, out_buf, in_buf, ssem, rsem):
        start, size = spans[part_id]
        value = pb[kz, :, start : start + size]
        for s, (direction, p, reach) in enumerate(STREAMS):
            if p == part_id:
                ring_arrive(s, reach - 1, size, in_buf, ssem, rsem)
                value = value + in_buf[BASE[s] + reach - 1, :, :size].astype(F32)
        return value

    def ring_round(j, part_ids, *buffers):
        for s, (_, p, reach) in enumerate(STREAMS):
            if j < reach and p in part_ids:
                ring_send(s, j, *buffers)

    first = (((0, half), (half, half)), snd, rcv, z1_s, z1_r)
    local[4].wait()
    theirs_wo = wo_vm.at[pl.ds(pl.multiple_of(other * wo_rows, 16), wo_rows)]
    arrive(theirs_wo, one_s.at[0], one_r.at[0], partner)
    for c in range(4):
        cols = slice(c * quarter, (c + 1) * quarter)
        block = jnp.dot(attn[...], wo_vm[:, cols], preferred_element_type=F32)
        pb[:, :, cols] = block.reshape(RING, ROWS, quarter)
        if c % 2 == 1:
            ring_round(0, (c // 2,), *first)
    issue("gu", 1)
    for j in range(1, 4):
        ring_round(j, (0, 1), *first)
    for p in range(2):
        resid[:, columns(p)] = ring_total(p, *first) + x_ref[:, columns(p)].astype(F32)
    gains = gain_ref[...].astype(F32)
    for n in range(gains.shape[0]):
        gain_row[:, n * 128 : (n + 1) * 128] = gains[n : n + 1]
    rows = resid[...]
    inverse = lax.rsqrt(jnp.mean(rows * rows, axis=-1, keepdims=True) + 1e-05)
    nb[kz] = (rows * inverse * gain_row[...]).astype(BF16)

    def chip_send(step, part_id):
        slot = part_id * RING + step % RING
        block = ring(step)
        send(
            nb.at[block, :, columns(part_id)], nb.at[RING + block, :, columns(part_id)],
            chip_s.at[slot], chip_r.at[slot], partner,
        )

    def gather_arrive(s, j):
        direction, part_id, _ = STREAMS[s]
        slot = BASE[s] + j
        step = -direction * (j + 1)
        arrive(nb.at[ring(step), :, columns(part_id)], zg_s.at[slot], zg_r.at[slot], (req, ring(-direction), core))

    def gather_send(s, j):
        direction, part_id, _ = STREAMS[s]
        slot = BASE[s] + j
        block = nb.at[ring(-direction * j), :, columns(part_id)]
        send(block, block, zg_s.at[slot], zg_r.at[slot], (req, ring(direction), core))

    order = (0, 2, 1, 3)
    for s in order:
        gather_send(s, 0)
    for p in range(2):
        chip_send(0, p)
    for j in range(1, 4):
        for s in order:
            direction, part_id, reach = STREAMS[s]
            gather_arrive(s, j - 1)
            if j < reach:
                gather_send(s, j)
            chip_send(-direction * j, part_id)
        if j == 2:
            issue("gu", 2)
    for s in (0, 1):
        direction, part_id, reach = STREAMS[s]
        gather_arrive(s, reach - 1)
        chip_send(-direction * reach, part_id)
    issue("gu", 3)
    issue("dt", 1)
    for index in range(len(PLAN)):
        land("gu", index)

    for c in range(4):
        if c % 2 == 0:
            for step in range(RING):
                slot = (c // 2) * RING + step
                block = nb.at[RING + ring(step), :, columns(c // 2)]
                arrive(block, chip_s.at[slot], chip_r.at[slot], partner)
        cols = slice(c * quarter, (c + 1) * quarter)
        value = jnp.dot(
            nb[:, :, cols].reshape(2 * RING * ROWS, quarter), gu_vm[cols, :], preferred_element_type=F32
        )
        if c == 0:
            acc[...] = value
        else:
            acc[...] += value
    gate, up = acc[:, :whole], acc[:, whole + 128 :]
    hid[:, :whole] = (gate / (1.0 + jnp.exp(-gate)) * up).astype(BF16)
    gate = acc[:, whole : whole + 128]
    up = pltpu.roll(gate, 64, 1)
    tail = (gate / (1.0 + jnp.exp(-gate)) * up).astype(BF16)
    hid[:, whole:] = tail[:, : units - whole]

    lead = EARLY * shard

    def unpack(place):
        start = place * packed
        rows = slice(place * shard, (place + 1) * shard)
        for n in range(whole // 128):
            dt_vm[rows, n * 128 : (n + 1) * 128] = raw[start + n * shard : start + (n + 1) * shard]
        tail = raw[start + packed - fold : start + packed]
        dt_vm[rows.start : rows.start + fold, whole:] = tail[:, : units - whole]
        tail = pltpu.roll(tail.astype(F32), 64, 1).astype(BF16)
        dt_vm[rows.start + fold : rows.stop, whole:] = tail[:, : units - whole]

    def multiply(spans, slot):
        for p, (start, size) in enumerate(spans):
            cols = slice(start, start + size)
            value = lax.dot_general(
                hid[...], dt_vm[cols, :], (((1,), (1,)), ((), ())), preferred_element_type=F32
            )
            pb[:, :, cols] = value[: RING * ROWS].reshape(RING, ROWS, size)
            xs[:, :, cols] = value[RING * ROWS :].astype(BF16).reshape(RING, ROWS, size)
            send(xs.at[:, :, cols], xr.at[:, :, cols], ex_s.at[slot + p], ex_r.at[slot + p], partner)

    def combine(part_id, spans, slot):
        start, size = spans[part_id]
        cols = slice(start, start + size)
        arrive(xr.at[:, :, cols], ex_s.at[slot + part_id], ex_r.at[slot + part_id], partner)
        pb[:, :, cols] += xr[:, :, cols].astype(F32)

    second = (((0, 1664), (1664, lead - 1664)), snd2, rcv2, z2_s, z2_r)
    third = (((lead, 1024), (lead + 1024, width - lead - 1024)), snd3, rcv3, z3_s, z3_r)
    issue("dt", 2)
    for index, entry in enumerate(PLAN):
        if entry[0] < 2:
            land("dt", index)
    for place in range(EARLY):
        unpack(place)
    multiply(second[0], 0)
    for p in range(2):
        combine(p, second[0], 0)
        ring_round(0, (p,), *second)
    issue("dt", 3)
    ring_round(1, (0, 1), *second)
    for index in range(len(PLAN)):
        land("dt", index)
    for place in range(EARLY, SIDE * SIDE):
        unpack(place)
    multiply(third[0], 2)
    ring_round(2, (0, 1), *second)
    for p in range(2):
        combine(p, third[0], 2)
        ring_round(0, (p,), *third)
    ring_round(3, (0, 1), *second)
    ring_round(1, (0, 1), *third)

    def finish(places, *buffers):
        for p, (start, size) in enumerate(buffers[0]):
            pb[0, :, start : start + size] = ring_total(p, *buffers)
        for place in places:
            start = place * shard
            skew = start % 128
            span = -(-(skew + shard) // 128) * 128
            block = pb[0, :, start - skew : start - skew + span]
            if skew:
                block = pltpu.roll(block, span - skew, 1)
            out_ref[plane(PLACES[place])] = block[:, :shard]

    ring_round(2, (0, 1), *third)
    ring_round(3, (0, 1), *third)
    finish(range(EARLY), *second)
    finish(range(EARLY, SIDE * SIDE), *third)
    for copy in saved:
        copy.wait()
    for copy in pending:
        copy.wait_send()


def layer(q, fresh_k, fresh_v, cosine, sine, length, table, x, gain, keys, values, wo, gate, up, down):
    width = x.shape[1]
    out_part, hidden = down.shape
    slots, head_dim = keys.shape
    pages = slots // 128
    tokens, heads = q.shape[0], q.shape[1] // head_dim
    vmem = pl.BlockSpec(memory_space=pltpu.VMEM)
    hbm = pl.BlockSpec(memory_space=pl.ANY)
    dma = pltpu.SemaphoreType.DMA
    part = pltpu.VMEM((heads, tokens // 2, 2 * head_dim), F32)
    hops = [pltpu.VMEM((SLOTS_Z, ROWS, size), BF16) for size in (width // 2, 1664, 1024)]
    plan = dma((len(PLAN),))
    packed = hidden * out_part // 128
    cache = jax.ShapeDtypeStruct(keys.shape, BF16)
    return pl.pallas_call(
        kernel,
        out_shape=(
            jax.ShapeDtypeStruct((SIDE * SIDE, ROWS, out_part), F32),
            jax.ShapeDtypeStruct(x.shape, F32),
            cache,
            cache,
        ),
        in_specs=[vmem] * 9 + [hbm] * 6,
        out_specs=(vmem, vmem, hbm, hbm),
        scratch_shapes=[
            pltpu.VMEM((2, heads, tokens // 2, head_dim), BF16),
            pltpu.VMEM((3 * 128, 2 * head_dim), F32),
            pltpu.VMEM((pages, 128), F32),
            pltpu.VMEM((1, slots), F32),
            pltpu.VMEM((slots, head_dim), BF16),
            pltpu.VMEM((slots, head_dim), BF16),
            pltpu.VMEM((2 * wo.shape[0], width), BF16),
            pltpu.VMEM(gate.shape, BF16),
            pltpu.VMEM(up.shape, BF16),
            pltpu.VMEM((width, 2 * hidden), BF16),
            pltpu.VMEM(down.shape, BF16),
            pltpu.VMEM((SIDE * SIDE * packed, 128), BF16),
            pltpu.VMEM((1, width), F32),
            pltpu.VMEM((width, hidden), BF16),
            part, part, part,
            pltpu.VMEM((tokens // 2, heads * head_dim), BF16),
            pltpu.VMEM((RING, ROWS, width), F32),
            pltpu.VMEM((2 * RING, ROWS, width), BF16),
            pltpu.VMEM((2 * RING * ROWS, 2 * hidden), F32),
            pltpu.VMEM((2 * RING * ROWS, hidden), BF16),
            hops[0], hops[0], hops[1], hops[1], hops[2], hops[2],
            pltpu.VMEM((RING, ROWS, width), BF16),
            pltpu.VMEM((RING, ROWS, width), BF16),
            dma((8,)),
            plan, plan, plan, plan,
            dma((2,)), dma((2,)),
            *[dma((SLOTS_Z,))] * 8,
            dma((2 * RING,)), dma((2 * RING,)),
            dma((4,)), dma((4,)),
        ],
        compiler_params=pltpu.CompilerParams(
            collective_id=0, has_side_effects=True, vmem_limit_bytes=62 * 2**20
        ),
        name="layer",
    )(q, fresh_k, fresh_v, cosine, sine, length, table, x, gain, keys, values, wo, gate, up, down)


def on_device(
    x_resid, q_new, k_new, v_new, k_cache, v_cache, cache_len, page_table, wo, norm_gain, w_gate, w_up, w_down
):
    new_tokens, head_dim = k_new.shape[1:]
    half = head_dim // 2
    positions = cache_len[0] + jnp.arange(new_tokens, dtype=jnp.int32)
    frequency = jnp.power(1000000.0, -2.0 * jnp.arange(half, dtype=F32) / head_dim)
    angles = positions.astype(F32)[:, None] * frequency[None, :]
    mlp, resid, keys, values = layer(
        q_new[0],
        k_new[0],
        v_new[0],
        jnp.cos(angles),
        jnp.sin(angles),
        cache_len[None],
        page_table,
        x_resid[0],
        norm_gain.reshape(-1, 128),
        k_cache.reshape(-1, head_dim),
        v_cache.reshape(-1, head_dim),
        wo,
        w_gate,
        w_up,
        w_down.T,
    )
    mlp = mlp.transpose(1, 0, 2).reshape(resid.shape)
    layer_out = (resid + mlp).astype(BF16)[None]
    return (layer_out, keys.reshape(k_cache.shape), values.reshape(v_cache.shape))


def solution(mesh):
    in_specs = (
        P("req", ("kv", "blk"), None),
        P("req", None, "kv"),
        P("req", None, "kv"),
        P("req", None, "kv"),
        P("req", "kv", "blk", None, None),
        P("req", "kv", "blk", None, None),
        P("req"),
        P("req", None),
        P(("kv", "blk"), None),
        P(),
        P("req", ("kv", "blk")),
        P("req", ("kv", "blk")),
        P(("kv", "blk"), "req"),
    )
    out_specs = (
        P("req", ("kv", "blk"), None),
        P("req", "kv", "blk", None, None),
        P("req", "kv", "blk", None, None),
    )
    return jax.shard_map(on_device, mesh=mesh, in_specs=in_specs, out_specs=out_specs, check_vma=False)
```
